256 devices in a mesh: pipe: 8 (over x, core), seq: 32 (over z, y).
Axes of the slice: x: 4, y: 4, z: 8, core: 2. Of those that a mesh axis runs over, the one named last changes fastest.
Arguments:
- saved_inputs: bfloat16 [8, 2, 8192, 1536], P('pipe', None, 'seq'), may hold values from -54 to 54
- arrived_grad: bfloat16 [8, 8192, 1536], P('pipe', 'seq'), may hold values from -6 to 6
- loss_grad: bfloat16 [1, 8192, 1536], P(None, 'seq'), may hold values from -6 to 6
- norm_gain: float32 [8, 1536], P('pipe'), may hold values from 0.25 to 1.75
- w_gate: bfloat16 [8, 384, 1536], P('pipe'), may hold values from -0.3125 to 0.3125
- w_value: bfloat16 [8, 384, 1536], P('pipe'), may hold values from -0.3125 to 0.3125
- w_out: bfloat16 [8, 384, 1536], P('pipe'), may hold values from -0.3125 to 0.3125
- r_factor: bfloat16 [8, 8192, 256], P('pipe', 'seq'), may hold values from -0.375 to 0.375
- l_factor: bfloat16 [8, 256, 1024], P('pipe', 'seq'), may hold values from -1 to 1
Outputs:
- sent_grad: bfloat16 [8, 2, 8192, 1536], P('pipe', None, 'seq')
The draws below stay inside these ranges and needn't reach their ends.
All inputs are finite; a program needn't handle non-finite values.
Results may differ from the reference program's by a relative error of at most 0.008.
Values may be sent and summed in bfloat16 or wider, within the bound.
A program may use at most 128 MiB of HBM per device.

```python
import math
import jax
import jax.numpy as jnp
from jax import lax

NBLK = 4
BSZ = 384
D = 1536
TOK_DEV = 256
TICKS = 2
SECTIONS = 8
SEQLEN = 8192
N_SEQ = 32


def draw_saved_inputs(key, part):
    key_base, key_column, key_row = jax.random.split(key, 3)
    shape_all = (SECTIONS, TICKS, SEQLEN, D)
    column_scale = jnp.exp(jax.random.uniform(key_column, (1, 1, 1, D), jnp.float32, math.log(0.3), math.log(3.0)))
    row_scale = jnp.exp(jax.random.uniform(key_row, (SECTIONS, TICKS, SEQLEN, 1), jnp.float32, math.log(0.3), math.log(3.0)))
    base_draw = jnp.clip(jax.random.normal(key_base, shape_all, jnp.float32), -6.0, 6.0)
    return (base_draw * column_scale * row_scale).astype(jnp.bfloat16)


def block_scale(rng, shape, shards, smallest, top_value):
    gain = 1.0
    for axis_at, blocks in shards:
        heights = jax.random.uniform(jax.random.fold_in(jax.random.fold_in(rng, 6), axis_at), (blocks,), jnp.float32, smallest / len(shards), top_value / len(shards))
        gain = gain * jnp.repeat(jnp.exp(heights), shape[axis_at] // blocks).reshape((-1,) + (1,) * (len(shape) - 1 - axis_at))
    return gain


def noise(rng, extent, width, bound, cuts=(), kind=jnp.bfloat16):
    entries = jax.random.normal(rng, extent, jnp.float32) * width
    if len(cuts) > 0:
        entries = block_scale(rng, extent, cuts, -0.22, 0.18) * entries
    return jnp.clip(entries, min=-bound, max=bound).astype(kind)


def setup_inputs(seed: int = 0) -> dict:
    seeds = jax.random.split(jax.random.key(seed), 10)
    return {
        "saved_inputs": draw_saved_inputs(jax.random.fold_in(seeds[9], 71), 0),
        "arrived_grad": noise(seeds[1], (SECTIONS, SEQLEN, D), 1.0, 6.0, ((0, 8), (1, 32))),
        "loss_grad": noise(seeds[2], (TICKS - 1, SEQLEN, D), 1.0, 6.0, ((1, 32),)),
        "norm_gain": jnp.clip(1.0 + 0.15 * jax.random.normal(seeds[3], (SECTIONS, D), jnp.float32), 0.25, 1.75),
        "w_gate": noise(seeds[4], (SECTIONS, BSZ, D), BSZ ** -0.5, 0.3125, ((0, 8),)),
        "w_value": noise(seeds[5], (SECTIONS, BSZ, D), BSZ ** -0.5, 0.3125, ((0, 8),)),
        "w_out": noise(seeds[6], (SECTIONS, BSZ, D), BSZ ** -0.5, 0.3125, ((0, 8),)),
        "r_factor": noise(seeds[7], (SECTIONS, SEQLEN, TOK_DEV), TOK_DEV ** -0.5, 0.375, ((0, 8), (1, 32))),
        "l_factor": noise(seeds[8], (SECTIONS, TOK_DEV, N_SEQ * N_SEQ), N_SEQ ** -0.5, 1.0, ((0, 8), (1, 32))),
    }


epsilon = 1e-05

def block_apply(rows_in, weight):
    row_count = rows_in.shape[0]
    left_blocks = rows_in.astype(jnp.float32).reshape(row_count, NBLK, BSZ)
    right_blocks = weight.astype(jnp.float32).reshape(BSZ, NBLK, BSZ)
    return jnp.einsum('rnc,cnb->rnb', left_blocks, right_blocks).reshape(row_count, NBLK * BSZ)

def block_back(rows_in, weight):
    row_count = rows_in.shape[0]
    left_blocks = rows_in.astype(jnp.float32).reshape(row_count, NBLK, BSZ)
    right_blocks = weight.astype(jnp.float32).reshape(BSZ, NBLK, BSZ)
    return jnp.einsum('rnb,cnb->rnc', left_blocks, right_blocks).reshape(row_count, NBLK * BSZ)

def section_backward(layer_in, out_grad, gain_row, gate_weight, value_weight, out_weight, r_section, l_section):
    inputs_f = layer_in.astype(jnp.float32)
    inv_scale = lax.rsqrt(lax.optimization_barrier(jnp.mean(inputs_f * inputs_f, axis=-1, keepdims=True)) + epsilon)
    normed = (inputs_f * inv_scale * gain_row).astype(jnp.bfloat16)
    gate_pre = block_apply(normed, gate_weight)
    values = block_apply(normed, value_weight).astype(jnp.bfloat16)
    r_blocks = r_section.astype(jnp.float32).reshape(N_SEQ, TOK_DEV, TOK_DEV)
    l_blocks = l_section.astype(jnp.float32).reshape(TOK_DEV, N_SEQ, N_SEQ)
    first_mix = jnp.einsum('ikj,ijd->ikd', r_blocks, values.astype(jnp.float32).reshape(N_SEQ, TOK_DEV, -1)).astype(jnp.bfloat16)
    seq_mixed = jnp.einsum('kpi,ikd->pkd', l_blocks, first_mix.astype(jnp.float32)).astype(jnp.bfloat16)
    seq_mixed = seq_mixed.reshape(N_SEQ * TOK_DEV, -1)
    inner_grad = block_back(out_grad, out_weight)
    gate_sigmoid = jax.nn.sigmoid(gate_pre)
    mixed_grad = (inner_grad * gate_pre * gate_sigmoid).astype(jnp.bfloat16)
    gate_grad = (inner_grad * seq_mixed.astype(jnp.float32) * gate_sigmoid * (1.0 + gate_pre * (1.0 - gate_sigmoid))).astype(jnp.bfloat16)
    folded = jnp.einsum('kpi,pkd->ikd', l_blocks, mixed_grad.astype(jnp.float32).reshape(N_SEQ, TOK_DEV, -1)).astype(jnp.bfloat16)
    value_grad = jnp.einsum('ikj,ikd->ijd', r_blocks, folded.astype(jnp.float32)).astype(jnp.bfloat16)
    value_grad = value_grad.reshape(N_SEQ * TOK_DEV, -1)
    norm_grad = (block_back(gate_grad, gate_weight) + block_back(value_grad, value_weight)) * gain_row
    result = out_grad.astype(jnp.float32) + inv_scale * norm_grad - inv_scale * inv_scale * inv_scale * inputs_f * lax.optimization_barrier(jnp.mean(norm_grad * inputs_f, axis=-1, keepdims=True))
    return result.astype(jnp.bfloat16)

def reference(saved_inputs, arrived_grad, loss_grad, norm_gain, w_gate, w_value, w_out, r_factor, l_factor):
    previous_sent = None
    per_tick = []
    for tick_index in range(TICKS):
        current = []
        for section_index in range(SECTIONS):
            if tick_index == 0:
                incoming = arrived_grad[section_index]
            elif section_index == SECTIONS - 1:
                incoming = loss_grad[tick_index - 1]
            else:
                incoming = previous_sent[section_index + 1]
            current.append(section_backward(saved_inputs[section_index, tick_index], incoming, norm_gain[section_index], w_gate[section_index], w_value[section_index], w_out[section_index], r_factor[section_index], l_factor[section_index]))
        previous_sent = current
        per_tick.append(jnp.stack(current))
    return jnp.stack(per_tick, axis=1)
```

```python
import functools

import jax
import jax.numpy as jnp
from jax import lax
from jax.experimental import pallas as pl
from jax.experimental.pallas import tpu as pltpu
from jax.sharding import PartitionSpec as P

TICKS = 2
NBLK = 4
MESH = pl.DeviceIdType.MESH
F32 = jnp.float32
BF16 = jnp.bfloat16

epsilon = 1e-05

A0, G0, M0, V0, A1, G1, M1, V1 = range(8)


def dot_nn(a, b):
    return lax.dot_general(a, b, (((1,), (0,)), ((), ())), preferred_element_type=F32)


def dot_nt(a, b):
    return lax.dot_general(a, b, (((1,), (1,)), ((), ())), preferred_element_type=F32)


def kernel(
    x_h, dy_h, lg_h, gain_h, wg_h, wv_h, wo_h, r_h, l_h, out_h,
    x_v, dy_v, lg_v, gain_v, wg_v, wv_v, wo_v, r_v, rt_v, l_v, lb_v, lbt_v,
    src, dst, coef, silu, slope, e_v, q_v, acc, res, dyn,
    load_sem, out_sem, send_sem, recv_sem, psend, precv,
):
    nseq = lax.axis_size("seq")
    npipe = lax.axis_size("pipe")
    me = lax.axis_index("seq")
    pi = lax.axis_index("pipe")
    before = lax.rem(pi + npipe - 1, npipe)
    after = lax.rem(pi + 1, npipe)
    width = wg_v.shape[0]
    rows = r_v.shape[0]
    per = rows // nseq
    model = gain_v.shape[1]

    pairs = (
        (x_h.at[0, 0], x_v.at[0]),
        (wv_h.at[0], wv_v),
        (r_h.at[0], r_v),
        (gain_h, gain_v),
        (wg_h.at[0], wg_v),
        (wo_h.at[0], wo_v),
        (dy_h.at[0], dy_v),
        (l_h.at[0], l_v),
        (x_h.at[0, 1], x_v.at[1]),
        (lg_h.at[0], lg_v),
    )
    loads = [pltpu.make_async_copy(a, b, load_sem.at[i]) for i, (a, b) in enumerate(pairs)]
    for c in loads:
        c.start()

    barrier = pltpu.get_barrier_semaphore()

    def greet(j, carry):
        pl.semaphore_signal(
            barrier, inc=1, device_id={"seq": lax.rem(me + j, nseq)}, device_id_type=MESH
        )
        return carry

    lax.fori_loop(1, nseq, greet, 0)
    for other in (before, after):
        pl.semaphore_signal(barrier, inc=1, device_id={"pipe": other}, device_id_type=MESH)

    def copy_to(a, n, peer):
        return pltpu.make_async_remote_copy(
            src_ref=src.at[a, n, peer],
            dst_ref=dst.at[a, n, me],
            send_sem=send_sem.at[a, n],
            recv_sem=recv_sem.at[a, n],
            device_id={"seq": peer},
            device_id_type=MESH,
        )

    def send(a, n):
        def body(j, carry):
            copy_to(a, n, lax.rem(me + j, nseq)).start()
            copy_to(a, n, lax.rem(me + nseq - j, nseq)).start()
            return carry

        lax.fori_loop(1, nseq // 2, body, 0)
        copy_to(a, n, lax.rem(me + nseq // 2, nseq)).start()
        dst[a, n, me] = src[a, n, me]

    def whole(a, n):
        return pltpu.make_async_remote_copy(
            src_ref=src.at[a, n, pl.ds(0, nseq - 1)],
            dst_ref=dst.at[a, n, pl.ds(0, nseq - 1)],
            send_sem=send_sem.at[a, n],
            recv_sem=recv_sem.at[a, n],
            device_id={"seq": lax.rem(me + 1, nseq)},
            device_id_type=MESH,
        )

    def put(a, n, value):
        src[a, n] = value.reshape(nseq, per, width).astype(BF16)

    def take(a, n):
        return dst[a, n].astype(F32).reshape(rows, width)

    def cols(n):
        return pl.ds(pl.multiple_of(n * width, 128), width)

    def each(body):
        def step(n, carry):
            body(n)
            return carry

        lax.fori_loop(0, NBLK, step, 0)

    def scale_of(t):
        total = jnp.zeros((rows, 1), F32)
        for n in range(NBLK):
            v = x_v[t, :, n * width : (n + 1) * width].astype(F32)
            total = total + jnp.sum(v * v, axis=-1, keepdims=True)
        q_v[t] = lax.rsqrt(total * (1.0 / model) + epsilon)

    def normed_of(t, n):
        return (x_v[t, :, cols(n)].astype(F32) * q_v[t] * gain_v[:, cols(n)]).astype(BF16)

    for i in range(4):
        loads[i].wait()
    scale_of(0)

    def front0(n):
        normed = normed_of(0, n)
        values = dot_nn(normed, wv_v[:, cols(n)]).astype(BF16)
        put(A0, n, dot_nn(r_v[...], values))

    def back0(n):
        normed = normed_of(0, n)
        gate = dot_nn(normed, wg_v[:, cols(n)])
        inner = dot_nt(dy_v[:, cols(n)], wo_v[:, cols(n)])
        sig = jax.nn.sigmoid(gate)
        put(G0, n, inner * gate * sig)
        coef[n] = inner * (sig * (1.0 + gate * (1.0 - sig)))

    front0(0)
    pl.semaphore_wait(barrier, nseq + 1)
    send(A0, 0)
    for i in range(4, 7):
        loads[i].wait()

    def start0(n):
        @pl.when(n > 0)
        def _():
            front0(n)
            send(A0, n)

        back0(n)
        send(G0, n)

    each(start0)

    loads[7].wait()
    rt_v[...] = r_v[...].astype(F32).T.astype(BF16)
    wide = l_v.shape[1]
    tiled = jnp.broadcast_to(l_v[...].astype(F32)[None], (nseq, per, wide)).reshape(rows, wide)
    row = lax.broadcasted_iota(jnp.int32, (rows, wide), 0)
    col = lax.broadcasted_iota(jnp.int32, (rows, wide), 1)
    own = jnp.where(col // nseq == row // per, tiled, 0.0).astype(BF16)
    col_c = lax.broadcasted_iota(jnp.int32, (wide, rows), 0)
    row_c = lax.broadcasted_iota(jnp.int32, (wide, rows), 1)
    spread = jnp.where(col_c % nseq == row_c // per, 1.0, 0.0).astype(BF16)
    big = dot_nn(own, spread)
    ra = lax.broadcasted_iota(jnp.int32, (rows, rows), 0)
    rb = lax.broadcasted_iota(jnp.int32, (rows, rows), 1)
    big = jnp.where(ra % per == rb % per, big, 0.0)
    lb_v[...] = big.astype(BF16)
    lbt_v[...] = big.T.astype(BF16)

    loads[8].wait()
    scale_of(1)

    def front1(n):
        normed = normed_of(1, n)
        values = dot_nn(normed, wv_v[:, cols(n)]).astype(BF16)
        put(A1, n, dot_nn(r_v[...], values))
        gate = dot_nn(normed, wg_v[:, cols(n)])
        sig = jax.nn.sigmoid(gate)
        silu[n] = gate * sig
        slope[n] = sig * (1.0 + gate * (1.0 - sig))

    each(front1)

    def mix(a, b, n):
        whole(a, n).wait_recv()
        put(b, n, dot_nn(lb_v[...], take(a, n).astype(BF16)))
        send(b, n)

    def fold(a, b, n):
        whole(a, n).wait_recv()
        put(b, n, dot_nn(lbt_v[...], take(a, n).astype(BF16)))
        send(b, n)

    def turn0(n):
        mix(A0, M0, n)
        fold(G0, V0, n)

    each(turn0)
    each(functools.partial(send, A1))

    def finish(t, m, v):
        acc[...] = jnp.zeros_like(acc)

        def part(n):
            whole(m, n).wait_recv()
            gate_grad = (coef[n] * take(m, n)).astype(BF16)
            left = dot_nt(gate_grad, wg_v[:, cols(n)])
            whole(v, n).wait_recv()
            value_grad = dot_nn(rt_v[...], take(v, n).astype(BF16)).astype(BF16)
            e = (left + dot_nt(value_grad, wv_v[:, cols(n)])) * gain_v[:, cols(n)]
            e_v[n] = e
            acc[...] += jnp.sum(e * x_v[t, :, cols(n)].astype(F32), axis=-1, keepdims=True)

        each(part)

    def result(t, n, dy):
        q = q_v[t]
        mean = acc[...] * (1.0 / model)
        value = dy.astype(F32) + q * e_v[n] - (q * q * q * mean) * x_v[t, :, cols(n)].astype(F32)
        res[t, n] = value.astype(BF16)

    def write(t, n):
        return pltpu.make_async_copy(res.at[t, n], out_h.at[0, t, :, cols(n)], out_sem.at[t, n])

    def passing(n):
        return pltpu.make_async_remote_copy(
            src_ref=res.at[0, n],
            dst_ref=dyn.at[n],
            send_sem=psend.at[n],
            recv_sem=precv.at[n],
            device_id={"pipe": before},
            device_id_type=MESH,
        )

    finish(0, M0, V0)

    def hand_on(n):
        result(0, n, dy_v[:, cols(n)])
        passing(n).start()
        write(0, n).start()

    each(hand_on)

    loads[9].wait()
    last = pi == npipe - 1

    def start1(n):
        passing(n).wait_recv()
        dy = jnp.where(last, lg_v[:, cols(n)].astype(F32), dyn[n].astype(F32)).astype(BF16)
        dy_v[:, cols(n)] = dy
        inner = dot_nt(dy, wo_v[:, cols(n)])
        put(G1, n, inner * silu[n])
        coef[n] = inner * slope[n]
        send(G1, n)
        mix(A1, M1, n)

    each(start1)
    each(functools.partial(fold, G1, V1))
    finish(1, M1, V1)

    def end(n):
        result(1, n, dy_v[:, cols(n)])
        write(1, n).start()

    each(end)

    def drain(n):
        for a in range(8):
            whole(a, n).wait_send()
        passing(n).wait_send()
        write(0, n).wait()
        write(1, n).wait()

    each(drain)


def local(*args):
    saved, _, _, _, w_gate, _, _, r_factor, l_factor = args
    _, ticks, rows, model = saved.shape
    width = w_gate.shape[1]
    nseq = lax.axis_size("seq")
    per = rows // nseq
    anywhere = pl.BlockSpec(memory_space=pl.ANY)
    vmem = pltpu.VMEM
    dma = pltpu.SemaphoreType.DMA
    return pl.pallas_call(
        kernel,
        out_shape=jax.ShapeDtypeStruct(saved.shape, BF16),
        in_specs=[anywhere] * len(args),
        out_specs=anywhere,
        scratch_shapes=[
            vmem((ticks, rows, model), BF16),
            vmem((rows, model), BF16),
            vmem((rows, model), BF16),
            vmem((1, model), F32),
            vmem((width, model), BF16),
            vmem((width, model), BF16),
            vmem((width, model), BF16),
            vmem((rows, rows), BF16),
            vmem((rows, rows), BF16),
            vmem(l_factor.shape[1:], BF16),
            vmem((rows, rows), BF16),
            vmem((rows, rows), BF16),
            vmem((8, NBLK, nseq, per, width), BF16),
            vmem((8, NBLK, nseq, per, width), BF16),
            vmem((NBLK, rows, width), F32),
            vmem((NBLK, rows, width), F32),
            vmem((NBLK, rows, width), F32),
            vmem((NBLK, rows, width), F32),
            vmem((ticks, rows, 1), F32),
            vmem((rows, 1), F32),
            vmem((ticks, NBLK, rows, width), BF16),
            vmem((NBLK, rows, width), BF16),
            dma((10,)),
            dma((ticks, NBLK)),
            dma((8, NBLK)),
            dma((8, NBLK)),
            dma((NBLK,)),
            dma((NBLK,)),
        ],
        compiler_params=pltpu.CompilerParams(
            collective_id=0, has_side_effects=True, vmem_limit_bytes=60 * 2**20
        ),
    )(*args)


def solution(mesh):
    placed = (
        P("pipe", None, "seq", None),
        P("pipe", "seq", None),
        P(None, "seq", None),
        P("pipe", None),
        P("pipe", None, None),
        P("pipe", None, None),
        P("pipe", None, None),
        P("pipe", "seq", None),
        P("pipe", "seq", None),
    )
    return jax.shard_map(
        local, mesh=mesh, in_specs=placed, out_specs=P("pipe", None, "seq", None), check_vma=False
    )
```

```python
import functools

import jax
import jax.numpy as jnp
from jax import lax
from jax.experimental import pallas as pl
from jax.experimental.pallas import tpu as pltpu
from jax.sharding import PartitionSpec as P

TICKS = 2
NBLK = 4
MESH = pl.DeviceIdType.MESH
F32 = jnp.float32
BF16 = jnp.bfloat16

epsilon = 1e-05

A0, G0, M0, V0, A1, G1, M1, V1 = range(8)


def dot_nn(a, b):
    return lax.dot_general(a, b, (((1,), (0,)), ((), ())), preferred_element_type=F32)


def dot_nt(a, b):
    return lax.dot_general(a, b, (((1,), (1,)), ((), ())), preferred_element_type=F32)


def kernel(
    x_h, dy_h, lg_h, gain_h, wg_h, wv_h, wo_h, r_h, l_h,
    out0, x1_v, base, weight,
    x0_v, dy_v, lg_v, gain_v, wg_v, wv_v, wo_v, r_v, rt_v, l_v, lb_v, lbt_v,
    src, dst, coef, silu, slope, q_v, acc, res, dyn,
    load_sem, send_sem, recv_sem, psend, precv,
):
    nseq = lax.axis_size("seq")
    npipe = lax.axis_size("pipe")
    me = lax.axis_index("seq")
    pi = lax.axis_index("pipe")
    before = lax.rem(pi + npipe - 1, npipe)
    after = lax.rem(pi + 1, npipe)
    width = wg_v.shape[0]
    rows = r_v.shape[0]
    per = rows // nseq
    model = gain_v.shape[1]

    x_v = (x0_v, x1_v)
    pairs = (
        (x_h.at[0, 0], x0_v),
        (wv_h.at[0], wv_v),
        (r_h.at[0], r_v),
        (gain_h, gain_v),
        (wg_h.at[0], wg_v),
        (wo_h.at[0], wo_v),
        (dy_h.at[0], dy_v),
        (l_h.at[0], l_v),
        (x_h.at[0, 1], x1_v),
        (lg_h.at[0], lg_v),
    )
    loads = [pltpu.make_async_copy(a, b, load_sem.at[i]) for i, (a, b) in enumerate(pairs)]
    for c in loads:
        c.start()

    barrier = pltpu.get_barrier_semaphore()

    def greet(j, carry):
        pl.semaphore_signal(
            barrier, inc=1, device_id={"seq": lax.rem(me + j, nseq)}, device_id_type=MESH
        )
        return carry

    lax.fori_loop(1, nseq, greet, 0)
    for other in (before, after):
        pl.semaphore_signal(barrier, inc=1, device_id={"pipe": other}, device_id_type=MESH)

    def copy_to(a, n, peer):
        return pltpu.make_async_remote_copy(
            src_ref=src.at[a, n, peer],
            dst_ref=dst.at[a, n, me],
            send_sem=send_sem.at[a, n],
            recv_sem=recv_sem.at[a, n],
            device_id={"seq": peer},
            device_id_type=MESH,
        )

    def send(a, n):
        def body(j, carry):
            copy_to(a, n, lax.rem(me + j, nseq)).start()
            copy_to(a, n, lax.rem(me + nseq - j, nseq)).start()
            return carry

        lax.fori_loop(1, nseq // 2, body, 0)
        copy_to(a, n, lax.rem(me + nseq // 2, nseq)).start()
        dst[a, n, me] = src[a, n, me]

    def whole(a, n):
        return pltpu.make_async_remote_copy(
            src_ref=src.at[a, n, pl.ds(0, nseq - 1)],
            dst_ref=dst.at[a, n, pl.ds(0, nseq - 1)],
            send_sem=send_sem.at[a, n],
            recv_sem=recv_sem.at[a, n],
            device_id={"seq": lax.rem(me + 1, nseq)},
            device_id_type=MESH,
        )

    def put(a, n, value):
        src[a, n] = value.reshape(nseq, per, width).astype(BF16)

    def take(a, n):
        return dst[a, n].astype(F32).reshape(rows, width)

    def cols(n):
        return pl.ds(pl.multiple_of(n * width, 128), width)

    def each(body):
        def step(n, carry):
            body(n)
            return carry

        lax.fori_loop(0, NBLK, step, 0)

    def scale_of(t):
        total = jnp.zeros((rows, 1), F32)
        for n in range(NBLK):
            v = x_v[t][:, n * width : (n + 1) * width].astype(F32)
            total = total + jnp.sum(v * v, axis=-1, keepdims=True)
        q_v[t] = lax.rsqrt(total * (1.0 / model) + epsilon)

    def normed_of(t, n):
        return (x_v[t][:, cols(n)].astype(F32) * q_v[t] * gain_v[:, cols(n)]).astype(BF16)

    for i in range(4):
        loads[i].wait()
    scale_of(0)

    def front0(n):
        normed = normed_of(0, n)
        values = dot_nn(normed, wv_v[:, cols(n)]).astype(BF16)
        put(A0, n, dot_nn(r_v[...], values))

    def back0(n):
        normed = normed_of(0, n)
        gate = dot_nn(normed, wg_v[:, cols(n)])
        inner = dot_nt(dy_v[:, cols(n)], wo_v[:, cols(n)])
        sig = jax.nn.sigmoid(gate)
        put(G0, n, inner * gate * sig)
        coef[n] = inner * (sig * (1.0 + gate * (1.0 - sig)))

    front0(0)
    pl.semaphore_wait(barrier, nseq + 1)
    send(A0, 0)
    for i in range(4, 7):
        loads[i].wait()

    def start0(n):
        @pl.when(n > 0)
        def _():
            front0(n)
            send(A0, n)

        back0(n)
        send(G0, n)

    each(start0)

    loads[7].wait()
    rt_v[...] = r_v[...].astype(F32).T.astype(BF16)
    wide = l_v.shape[1]
    tiled = jnp.broadcast_to(l_v[...].astype(F32)[None], (nseq, per, wide)).reshape(rows, wide)
    row = lax.broadcasted_iota(jnp.int32, (rows, wide), 0)
    col = lax.broadcasted_iota(jnp.int32, (rows, wide), 1)
    own = jnp.where(col // nseq == row // per, tiled, 0.0).astype(BF16)
    col_c = lax.broadcasted_iota(jnp.int32, (wide, rows), 0)
    row_c = lax.broadcasted_iota(jnp.int32, (wide, rows), 1)
    spread = jnp.where(col_c % nseq == row_c // per, 1.0, 0.0).astype(BF16)
    big = dot_nn(own, spread)
    ra = lax.broadcasted_iota(jnp.int32, (rows, rows), 0)
    rb = lax.broadcasted_iota(jnp.int32, (rows, rows), 1)
    big = jnp.where(ra % per == rb % per, big, 0.0)
    lb_v[...] = big.astype(BF16)
    lbt_v[...] = big.T.astype(BF16)

    loads[8].wait()
    scale_of(1)

    def front1(n):
        normed = normed_of(1, n)
        values = dot_nn(normed, wv_v[:, cols(n)]).astype(BF16)
        put(A1, n, dot_nn(r_v[...], values))
        gate = dot_nn(normed, wg_v[:, cols(n)])
        sig = jax.nn.sigmoid(gate)
        silu[n] = gate * sig
        slope[n] = sig * (1.0 + gate * (1.0 - sig))

    each(front1)

    def mix(a, b, n):
        whole(a, n).wait_recv()
        put(b, n, dot_nn(lb_v[...], take(a, n).astype(BF16)))
        send(b, n)

    def fold(a, b, n):
        whole(a, n).wait_recv()
        put(b, n, dot_nn(lbt_v[...], take(a, n).astype(BF16)))
        send(b, n)

    def turn0(n):
        mix(A0, M0, n)
        fold(G0, V0, n)

    each(turn0)
    each(functools.partial(send, A1))

    def finish(t, m, v):
        acc[...] = jnp.zeros_like(acc)

        def part(n):
            whole(m, n).wait_recv()
            gate_grad = (coef[n] * take(m, n)).astype(BF16)
            left = dot_nt(gate_grad, wg_v[:, cols(n)])
            whole(v, n).wait_recv()
            value_grad = dot_nn(rt_v[...], take(v, n).astype(BF16)).astype(BF16)
            e = (left + dot_nt(value_grad, wv_v[:, cols(n)])) * gain_v[:, cols(n)]
            base[n] = dy_v[:, cols(n)].astype(F32) + q_v[t] * e
            acc[...] += jnp.sum(e * x_v[t][:, cols(n)].astype(F32), axis=-1, keepdims=True)

        each(part)
        q = q_v[t]
        acc[...] = q * q * q * (acc[...] * (1.0 / model))

    def passing(n):
        return pltpu.make_async_remote_copy(
            src_ref=res.at[n],
            dst_ref=dyn.at[n],
            send_sem=psend.at[n],
            recv_sem=precv.at[n],
            device_id={"pipe": before},
            device_id_type=MESH,
        )

    finish(0, M0, V0)

    def hand_on(n):
        value = (base[n] - acc[...] * x0_v[:, cols(n)].astype(F32)).astype(BF16)
        res[n] = value
        passing(n).start()
        out0[:, cols(n)] = value

    each(hand_on)

    loads[9].wait()
    last = pi == npipe - 1

    def start1(n):
        passing(n).wait_recv()
        dy = jnp.where(last, lg_v[:, cols(n)].astype(F32), dyn[n].astype(F32)).astype(BF16)
        dy_v[:, cols(n)] = dy
        inner = dot_nt(dy, wo_v[:, cols(n)])
        put(G1, n, inner * silu[n])
        coef[n] = inner * slope[n]
        send(G1, n)
        mix(A1, M1, n)

    each(start1)
    each(functools.partial(fold, G1, V1))

    def drain(a, n):
        whole(a, n).wait_send()

    for a in range(7):
        each(functools.partial(drain, a))
    each(lambda n: passing(n).wait_send())
    finish(1, M1, V1)
    weight[...] = jnp.broadcast_to(acc[...], weight.shape)
    each(functools.partial(drain, V1))


def closing(out0, x1_v, base, weight, out_h, res, out_sem):
    width = base.shape[2]
    first = pltpu.make_async_copy(out0, out_h.at[0, 0], out_sem.at[NBLK])
    first.start()
    copies = []
    for n in range(NBLK):
        span = pl.ds(n * width, width)
        value = base[n] - weight[:, :1] * x1_v[:, span].astype(F32)
        res[n] = value.astype(BF16)
        copies.append(pltpu.make_async_copy(res.at[n], out_h.at[0, 1, :, span], out_sem.at[n]))
        copies[-1].start()
    for c in copies:
        c.wait()
    first.wait()


def local(*args):
    saved, _, _, _, w_gate, _, _, r_factor, l_factor = args
    _, ticks, rows, model = saved.shape
    width = w_gate.shape[1]
    nseq = lax.axis_size("seq")
    per = rows // nseq
    anywhere = pl.BlockSpec(memory_space=pl.ANY)
    vmem = pltpu.VMEM
    dma = pltpu.SemaphoreType.DMA
    parts = pl.pallas_call(
        kernel,
        out_shape=(
            vmem((rows, model), BF16),
            vmem((rows, model), BF16),
            vmem((NBLK, rows, width), F32),
            vmem((rows, 128), F32),
        ),
        in_specs=[anywhere] * len(args),
        out_specs=(pl.BlockSpec(memory_space=vmem),) * 4,
        scratch_shapes=[
            vmem((rows, model), BF16),
            vmem((rows, model), BF16),
            vmem((rows, model), BF16),
            vmem((1, model), F32),
            vmem((width, model), BF16),
            vmem((width, model), BF16),
            vmem((width, model), BF16),
            vmem((rows, rows), BF16),
            vmem((rows, rows), BF16),
            vmem(l_factor.shape[1:], BF16),
            vmem((rows, rows), BF16),
            vmem((rows, rows), BF16),
            vmem((8, NBLK, nseq, per, width), BF16),
            vmem((8, NBLK, nseq, per, width), BF16),
            vmem((NBLK, rows, width), F32),
            vmem((NBLK, rows, width), F32),
            vmem((NBLK, rows, width), F32),
            vmem((ticks, rows, 1), F32),
            vmem((rows, 1), F32),
            vmem((NBLK, rows, width), BF16),
            vmem((NBLK, rows, width), BF16),
            dma((10,)),
            dma((8, NBLK)),
            dma((8, NBLK)),
            dma((NBLK,)),
            dma((NBLK,)),
        ],
        compiler_params=pltpu.CompilerParams(
            collective_id=0, has_side_effects=True, vmem_limit_bytes=60 * 2**20
        ),
    )(*args)
    return pl.pallas_call(
        closing,
        out_shape=jax.ShapeDtypeStruct(saved.shape, BF16),
        in_specs=[pl.BlockSpec(memory_space=vmem)] * 4,
        out_specs=anywhere,
        scratch_shapes=[vmem((NBLK, rows, width), BF16), dma((NBLK + 1,))],
        compiler_params=pltpu.CompilerParams(vmem_limit_bytes=16 * 2**20),
    )(*parts)


def solution(mesh):
    placed = (
        P("pipe", None, "seq", None),
        P("pipe", "seq", None),
        P(None, "seq", None),
        P("pipe", None),
        P("pipe", None, None),
        P("pipe", None, None),
        P("pipe", None, None),
        P("pipe", "seq", None),
        P("pipe", "seq", None),
    )
    return jax.shard_map(
        local, mesh=mesh, in_specs=placed, out_specs=P("pipe", None, "seq", None), check_vma=False
    )
```

```python
import functools

import jax
import jax.numpy as jnp
from jax import lax
from jax.experimental import pallas as pl
from jax.experimental.pallas import tpu as pltpu
from jax.sharding import PartitionSpec as P

TICKS = 2
NBLK = 4
HELD = 2
MESH = pl.DeviceIdType.MESH
F32 = jnp.float32
BF16 = jnp.bfloat16

epsilon = 1e-05

A0, G0, M0, V0, A1, G1, M1, V1 = range(8)


def dot_nn(a, b):
    return lax.dot_general(a, b, (((1,), (0,)), ((), ())), preferred_element_type=F32)


def dot_nt(a, b):
    return lax.dot_general(a, b, (((1,), (1,)), ((), ())), preferred_element_type=F32)


def kernel(
    x_h, dy_h, lg_h, gain_h, wg_h, wv_h, wo_h, r_h, l_h,
    out0, x1_v, base, weight,
    x0_v, dy_v, lg_v, gain_v, wg_v, wv_v, wo_v, r_v, rt_v, l_v, lb_v, lbt_v,
    src, dst, coef, silu, slope, side, q_v, acc, res, dyn,
    load_sem, send_sem, recv_sem, psend, precv,
):
    nseq = lax.axis_size("seq")
    npipe = lax.axis_size("pipe")
    me = lax.axis_index("seq")
    pi = lax.axis_index("pipe")
    before = lax.rem(pi + npipe - 1, npipe)
    after = lax.rem(pi + 1, npipe)
    width = wg_v.shape[0]
    rows = r_v.shape[0]
    per = rows // nseq
    model = gain_v.shape[1]

    x_v = (x0_v, x1_v)
    pairs = (
        (x_h.at[0, 0], x0_v),
        (wv_h.at[0], wv_v),
        (r_h.at[0], r_v),
        (gain_h, gain_v),
        (wg_h.at[0], wg_v),
        (wo_h.at[0], wo_v),
        (dy_h.at[0], dy_v),
        (l_h.at[0], l_v),
        (x_h.at[0, 1], x1_v),
        (lg_h.at[0], lg_v),
    )
    loads = [pltpu.make_async_copy(a, b, load_sem.at[i]) for i, (a, b) in enumerate(pairs)]
    for c in loads[:4]:
        c.start()

    barrier = pltpu.get_barrier_semaphore()

    for d in range(nseq // 2, 0, -1):
        for peer in sorted({(nseq + d) % nseq, (nseq - d) % nseq}):
            pl.semaphore_signal(
                barrier, inc=1, device_id={"seq": lax.rem(me + peer, nseq)}, device_id_type=MESH
            )
    for other in (before, after):
        pl.semaphore_signal(barrier, inc=1, device_id={"pipe": other}, device_id_type=MESH)
    for c in loads[4:]:
        c.start()

    def copy_to(a, n, peer):
        return pltpu.make_async_remote_copy(
            src_ref=src.at[a, n, peer],
            dst_ref=dst.at[a, n, me],
            send_sem=send_sem.at[a, n],
            recv_sem=recv_sem.at[a, n],
            device_id={"seq": peer},
            device_id_type=MESH,
        )

    def send(a, n):
        half = nseq // 2
        copy_to(a, n, lax.rem(me + half, nseq)).start()

        def body(j, carry):
            copy_to(a, n, lax.rem(me + half + j, nseq)).start()
            copy_to(a, n, lax.rem(me + half - j, nseq)).start()
            return carry

        lax.fori_loop(1, half, body, 0)
        dst[a, n, me] = src[a, n, me]

    def whole(a, n):
        return pltpu.make_async_remote_copy(
            src_ref=src.at[a, n, pl.ds(0, nseq - 1)],
            dst_ref=dst.at[a, n, pl.ds(0, nseq - 1)],
            send_sem=send_sem.at[a, n],
            recv_sem=recv_sem.at[a, n],
            device_id={"seq": lax.rem(me + 1, nseq)},
            device_id_type=MESH,
        )

    def put(a, n, value):
        src[a, n] = value.reshape(nseq, per, width).astype(BF16)

    def take(a, n):
        return dst[a, n].astype(F32).reshape(rows, width)

    def cols(n):
        return pl.ds(pl.multiple_of(n * width, 128), width)

    def each(body, first=0):
        def step(n, carry):
            body(n)
            return carry

        lax.fori_loop(first, NBLK, step, 0)

    def scale_of(t):
        total = jnp.zeros((rows, 1), F32)
        for n in range(NBLK):
            v = x_v[t][:, n * width : (n + 1) * width].astype(F32)
            total = total + jnp.sum(v * v, axis=-1, keepdims=True)
        q_v[t] = lax.rsqrt(total * (1.0 / model) + epsilon)

    def normed_of(t, n):
        return (x_v[t][:, cols(n)].astype(F32) * q_v[t] * gain_v[:, cols(n)]).astype(BF16)

    for i in range(4):
        loads[i].wait()
    scale_of(0)

    def front0(n):
        normed = normed_of(0, n)
        values = dot_nn(normed, wv_v[:, cols(n)]).astype(BF16)
        put(A0, n, dot_nn(r_v[...], values))

    def back0(n):
        normed = normed_of(0, n)
        gate = dot_nn(normed, wg_v[:, cols(n)])
        inner = dot_nt(dy_v[:, cols(n)], wo_v[:, cols(n)])
        sig = jax.nn.sigmoid(gate)
        put(G0, n, inner * gate * sig)
        coef[n] = inner * (sig * (1.0 + gate * (1.0 - sig)))

    front0(0)
    pl.semaphore_wait(barrier, nseq + 1)
    send(A0, 0)
    for i in range(4, 7):
        loads[i].wait()

    def start0(n):
        @pl.when(n > 0)
        def _():
            front0(n)
            send(A0, n)

        back0(n)
        send(G0, n)

    each(start0)

    loads[7].wait()
    rt_v[...] = r_v[...].astype(F32).T.astype(BF16)
    wide = l_v.shape[1]
    tiled = jnp.broadcast_to(l_v[...].astype(F32)[None], (nseq, per, wide)).reshape(rows, wide)
    row = lax.broadcasted_iota(jnp.int32, (rows, wide), 0)
    col = lax.broadcasted_iota(jnp.int32, (rows, wide), 1)
    own = jnp.where(col // nseq == row // per, tiled, 0.0).astype(BF16)
    col_c = lax.broadcasted_iota(jnp.int32, (wide, rows), 0)
    row_c = lax.broadcasted_iota(jnp.int32, (wide, rows), 1)
    spread = jnp.where(col_c % nseq == row_c // per, 1.0, 0.0).astype(BF16)
    big = dot_nn(own, spread)
    ra = lax.broadcasted_iota(jnp.int32, (rows, rows), 0)
    rb = lax.broadcasted_iota(jnp.int32, (rows, rows), 1)
    big = jnp.where(ra % per == rb % per, big, 0.0)
    lb_v[...] = big.astype(BF16)
    lbt_v[...] = big.T.astype(BF16)

    loads[8].wait()
    scale_of(1)

    def front1(n):
        normed = normed_of(1, n)
        values = dot_nn(normed, wv_v[:, cols(n)]).astype(BF16)
        put(A1, n, dot_nn(r_v[...], values))
        gate = dot_nn(normed, wg_v[:, cols(n)])
        sig = jax.nn.sigmoid(gate)
        silu[n] = gate * sig
        slope[n] = sig * (1.0 + gate * (1.0 - sig))

    each(front1)

    def mix(a, b, n):
        whole(a, n).wait_recv()
        put(b, n, dot_nn(lb_v[...], take(a, n).astype(BF16)))
        send(b, n)

    def fold(a, b, n):
        whole(a, n).wait_recv()
        put(b, n, dot_nn(lbt_v[...], take(a, n).astype(BF16)))
        send(b, n)

    def turn0(n):
        mix(A0, M0, n)
        fold(G0, V0, n)

    each(turn0)
    each(functools.partial(send, A1))

    def finish(t, m, v):
        acc[...] = jnp.zeros_like(acc)

        def part(n):
            whole(v, n).wait_recv()
            value_grad = dot_nn(rt_v[...], take(v, n).astype(BF16)).astype(BF16)
            side[...] = dot_nt(value_grad, wv_v[:, cols(n)])
            whole(m, n).wait_recv()
            gate_grad = (coef[n] * take(m, n)).astype(BF16)
            e = (dot_nt(gate_grad, wg_v[:, cols(n)]) + side[...]) * gain_v[:, cols(n)]
            base[n] = dy_v[:, cols(n)].astype(F32) + q_v[t] * e
            acc[...] += jnp.sum(e * x_v[t][:, cols(n)].astype(F32), axis=-1, keepdims=True)

        each(part)
        q = q_v[t]
        acc[...] = q * q * q * (acc[...] * (1.0 / model))

    def passing(n):
        return pltpu.make_async_remote_copy(
            src_ref=res.at[n],
            dst_ref=dyn.at[n],
            send_sem=psend.at[n],
            recv_sem=precv.at[n],
            device_id={"pipe": before},
            device_id_type=MESH,
        )

    finish(0, M0, V0)

    def hand_on(n):
        value = (base[n] - acc[...] * x0_v[:, cols(n)].astype(F32)).astype(BF16)
        res[n] = value
        passing(n).start()
        out0[:, cols(n)] = value

    each(hand_on)

    loads[9].wait()
    last = pi == npipe - 1

    def start1(n):
        passing(n).wait_recv()
        dy = jnp.where(last, lg_v[:, cols(n)].astype(F32), dyn[n].astype(F32)).astype(BF16)
        dy_v[:, cols(n)] = dy
        inner = dot_nt(dy, wo_v[:, cols(n)])
        put(G1, n, inner * silu[n])
        coef[n] = inner * slope[n]
        send(G1, n)

        @pl.when(n < NBLK - HELD)
        def _():
            mix(A1, M1, n)

    each(start1)
    each(functools.partial(fold, G1, V1))
    each(functools.partial(mix, A1, M1), NBLK - HELD)

    def drain(a, n):
        whole(a, n).wait_send()

    for a in (A0, G0, M0, V0, A1, G1, V1):
        each(functools.partial(drain, a))
    each(lambda n: passing(n).wait_send())
    finish(1, M1, V1)
    weight[...] = jnp.broadcast_to(acc[...], weight.shape)
    each(functools.partial(drain, M1))


def closing(out0, x1_v, base, weight, out_h, res, out_sem):
    width = base.shape[2]
    first = pltpu.make_async_copy(out0, out_h.at[0, 0], out_sem.at[NBLK])
    first.start()
    copies = []
    for n in range(NBLK):
        span = pl.ds(n * width, width)
        value = base[n] - weight[:, :1] * x1_v[:, span].astype(F32)
        res[n] = value.astype(BF16)
        copies.append(pltpu.make_async_copy(res.at[n], out_h.at[0, 1, :, span], out_sem.at[n]))
        copies[-1].start()
    for c in copies:
        c.wait()
    first.wait()


def local(*args):
    saved, _, _, _, w_gate, _, _, r_factor, l_factor = args
    _, ticks, rows, model = saved.shape
    width = w_gate.shape[1]
    nseq = lax.axis_size("seq")
    per = rows // nseq
    anywhere = pl.BlockSpec(memory_space=pl.ANY)
    vmem = pltpu.VMEM
    dma = pltpu.SemaphoreType.DMA
    parts = pl.pallas_call(
        kernel,
        out_shape=(
            vmem((rows, model), BF16),
            vmem((rows, model), BF16),
            vmem((NBLK, rows, width), F32),
            vmem((rows, 128), F32),
        ),
        in_specs=[anywhere] * len(args),
        out_specs=(pl.BlockSpec(memory_space=vmem),) * 4,
        scratch_shapes=[
            vmem((rows, model), BF16),
            vmem((rows, model), BF16),
            vmem((rows, model), BF16),
            vmem((1, model), F32),
            vmem((width, model), BF16),
            vmem((width, model), BF16),
            vmem((width, model), BF16),
            vmem((rows, rows), BF16),
            vmem((rows, rows), BF16),
            vmem(l_factor.shape[1:], BF16),
            vmem((rows, rows), BF16),
            vmem((rows, rows), BF16),
            vmem((8, NBLK, nseq, per, width), BF16),
            vmem((8, NBLK, nseq, per, width), BF16),
            vmem((NBLK, rows, width), F32),
            vmem((NBLK, rows, width), F32),
            vmem((NBLK, rows, width), F32),
            vmem((rows, width), F32),
            vmem((ticks, rows, 1), F32),
            vmem((rows, 1), F32),
            vmem((NBLK, rows, width), BF16),
            vmem((NBLK, rows, width), BF16),
            dma((10,)),
            dma((8, NBLK)),
            dma((8, NBLK)),
            dma((NBLK,)),
            dma((NBLK,)),
        ],
        compiler_params=pltpu.CompilerParams(
            collective_id=0, has_side_effects=True, vmem_limit_bytes=60 * 2**20
        ),
    )(*args)
    return pl.pallas_call(
        closing,
        out_shape=jax.ShapeDtypeStruct(saved.shape, BF16),
        in_specs=[pl.BlockSpec(memory_space=vmem)] * 4,
        out_specs=anywhere,
        scratch_shapes=[vmem((NBLK, rows, width), BF16), dma((NBLK + 1,))],
        compiler_params=pltpu.CompilerParams(vmem_limit_bytes=16 * 2**20),
    )(*parts)


def solution(mesh):
    placed = (
        P("pipe", None, "seq", None),
        P("pipe", "seq", None),
        P(None, "seq", None),
        P("pipe", None),
        P("pipe", None, None),
        P("pipe", None, None),
        P("pipe", None, None),
        P("pipe", "seq", None),
        P("pipe", "seq", None),
    )
    return jax.shard_map(
        local, mesh=mesh, in_specs=placed, out_specs=P("pipe", None, "seq", None), check_vma=False
    )
```

```python
import functools

import jax
import jax.numpy as jnp
from jax import lax
from jax.experimental import pallas as pl
from jax.experimental.pallas import tpu as pltpu
from jax.sharding import PartitionSpec as P

TICKS = 2
NBLK = 4
HELD = 2
MESH = pl.DeviceIdType.MESH
F32 = jnp.float32
BF16 = jnp.bfloat16

epsilon = 1e-05

A0, G0, M0, V0, A1, G1, M1, V1 = range(8)


def dot_nn(a, b):
    return lax.dot_general(a, b, (((1,), (0,)), ((), ())), preferred_element_type=F32)


def dot_nt(a, b):
    return lax.dot_general(a, b, (((1,), (1,)), ((), ())), preferred_element_type=F32)


def kernel(
    x_h, dy_h, lg_h, gain_h, wg_h, wv_h, wo_h, r_h, l_h,
    out0, x1_v, base, weight,
    x0_v, dy_v, lg_v, gain_v, wg_v, wv_v, wo_v, r_v, rt_v, l_v, lb_v, lbt_v,
    src, dst, coef, silu, slope, side, gx, qg, q_v, acc, res, dyn,
    load_sem, send_sem, recv_sem, psend, precv,
):
    nseq = lax.axis_size("seq")
    npipe = lax.axis_size("pipe")
    me = lax.axis_index("seq")
    pi = lax.axis_index("pipe")
    before = lax.rem(pi + npipe - 1, npipe)
    after = lax.rem(pi + 1, npipe)
    width = wg_v.shape[0]
    rows = r_v.shape[0]
    per = rows // nseq
    model = gain_v.shape[1]

    x_v = (x0_v, x1_v)
    pairs = (
        (x_h.at[0, 0], x0_v),
        (wv_h.at[0], wv_v),
        (r_h.at[0], r_v),
        (gain_h, gain_v),
        (wg_h.at[0], wg_v),
        (wo_h.at[0], wo_v),
        (dy_h.at[0], dy_v),
        (l_h.at[0], l_v),
        (x_h.at[0, 1], x1_v),
        (lg_h.at[0], lg_v),
    )
    loads = [pltpu.make_async_copy(a, b, load_sem.at[i]) for i, (a, b) in enumerate(pairs)]
    for c in loads[:4]:
        c.start()

    barrier = pltpu.get_barrier_semaphore()

    for d in range(nseq // 2, 0, -1):
        for peer in sorted({(nseq + d) % nseq, (nseq - d) % nseq}):
            pl.semaphore_signal(
                barrier, inc=1, device_id={"seq": lax.rem(me + peer, nseq)}, device_id_type=MESH
            )
    for other in (before, after):
        pl.semaphore_signal(barrier, inc=1, device_id={"pipe": other}, device_id_type=MESH)
    for c in loads[4:]:
        c.start()

    def copy_to(a, n, peer):
        return pltpu.make_async_remote_copy(
            src_ref=src.at[a, n, peer],
            dst_ref=dst.at[a, n, me],
            send_sem=send_sem.at[a, n],
            recv_sem=recv_sem.at[a, n],
            device_id={"seq": peer},
            device_id_type=MESH,
        )

    def send(a, n):
        half = nseq // 2
        copy_to(a, n, lax.rem(me + half, nseq)).start()

        def body(j, carry):
            copy_to(a, n, lax.rem(me + half + j, nseq)).start()
            copy_to(a, n, lax.rem(me + half - j, nseq)).start()
            return carry

        lax.fori_loop(1, half, body, 0)
        dst[a, n, me] = src[a, n, me]

    def whole(a, n):
        return pltpu.make_async_remote_copy(
            src_ref=src.at[a, n, pl.ds(0, nseq - 1)],
            dst_ref=dst.at[a, n, pl.ds(0, nseq - 1)],
            send_sem=send_sem.at[a, n],
            recv_sem=recv_sem.at[a, n],
            device_id={"seq": lax.rem(me + 1, nseq)},
            device_id_type=MESH,
        )

    def put(a, n, value):
        src[a, n] = value.reshape(nseq, per, width).astype(BF16)

    def take(a, n):
        return dst[a, n].astype(F32).reshape(rows, width)

    def cols(n):
        return pl.ds(pl.multiple_of(n * width, 128), width)

    def each(body, first=0):
        def step(n, carry):
            body(n)
            return carry

        lax.fori_loop(first, NBLK, step, 0)

    def scale_of(t):
        total = jnp.zeros((rows, 1), F32)
        for n in range(NBLK):
            v = x_v[t][:, n * width : (n + 1) * width].astype(F32)
            total = total + jnp.sum(v * v, axis=-1, keepdims=True)
        q_v[t] = lax.rsqrt(total * (1.0 / model) + epsilon)

    def normed_of(t, n):
        return (x_v[t][:, cols(n)].astype(F32) * q_v[t] * gain_v[:, cols(n)]).astype(BF16)

    for i in range(4):
        loads[i].wait()
    scale_of(0)

    def front0(n):
        normed = normed_of(0, n)
        values = dot_nn(normed, wv_v[:, cols(n)]).astype(BF16)
        put(A0, n, dot_nn(r_v[...], values))

    def back0(n):
        normed = normed_of(0, n)
        gate = dot_nn(normed, wg_v[:, cols(n)])
        inner = dot_nt(dy_v[:, cols(n)], wo_v[:, cols(n)])
        sig = jax.nn.sigmoid(gate)
        put(G0, n, inner * gate * sig)
        coef[n] = inner * (sig * (1.0 + gate * (1.0 - sig)))

    front0(0)
    pl.semaphore_wait(barrier, nseq + 1)
    send(A0, 0)
    for i in range(4, 7):
        loads[i].wait()

    def start0(n):
        @pl.when(n > 0)
        def _():
            front0(n)
            send(A0, n)

        back0(n)
        send(G0, n)

    each(start0)

    loads[7].wait()
    rt_v[...] = r_v[...].astype(F32).T.astype(BF16)
    wide = l_v.shape[1]
    tiled = jnp.broadcast_to(l_v[...].astype(F32)[None], (nseq, per, wide)).reshape(rows, wide)
    row = lax.broadcasted_iota(jnp.int32, (rows, wide), 0)
    col = lax.broadcasted_iota(jnp.int32, (rows, wide), 1)
    own = jnp.where(col // nseq == row // per, tiled, 0.0).astype(BF16)
    col_c = lax.broadcasted_iota(jnp.int32, (wide, rows), 0)
    row_c = lax.broadcasted_iota(jnp.int32, (wide, rows), 1)
    spread = jnp.where(col_c % nseq == row_c // per, 1.0, 0.0).astype(BF16)
    big = dot_nn(own, spread)
    ra = lax.broadcasted_iota(jnp.int32, (rows, rows), 0)
    rb = lax.broadcasted_iota(jnp.int32, (rows, rows), 1)
    big = jnp.where(ra % per == rb % per, big, 0.0)
    lb_v[...] = big.astype(BF16)
    lbt_v[...] = big.T.astype(BF16)

    loads[8].wait()
    scale_of(1)

    def front1(n):
        normed = normed_of(1, n)
        values = dot_nn(normed, wv_v[:, cols(n)]).astype(BF16)
        put(A1, n, dot_nn(r_v[...], values))
        gate = dot_nn(normed, wg_v[:, cols(n)])
        sig = jax.nn.sigmoid(gate)
        silu[n] = gate * sig
        slope[n] = sig * (1.0 + gate * (1.0 - sig))

    each(front1)

    def mix(a, b, n):
        whole(a, n).wait_recv()
        put(b, n, dot_nn(lb_v[...], take(a, n).astype(BF16)))
        send(b, n)

    def fold(a, b, n):
        whole(a, n).wait_recv()
        put(b, n, dot_nn(lbt_v[...], take(a, n).astype(BF16)))
        send(b, n)

    def turn0(n):
        mix(A0, M0, n)
        fold(G0, V0, n)

    each(turn0)
    each(functools.partial(send, A1))

    def finish(t, m, v):
        acc[...] = jnp.zeros_like(acc)

        def part(n):
            whole(v, n).wait_recv()
            value_grad = dot_nn(rt_v[...], take(v, n).astype(BF16)).astype(BF16)
            side[...] = dot_nt(value_grad, wv_v[:, cols(n)])
            scaled = gain_v[:, cols(n)] * x_v[t][:, cols(n)].astype(F32)
            gx[...] = scaled
            acc[...] += jnp.sum(side[...] * scaled, axis=-1, keepdims=True)
            qg[...] = q_v[t] * gain_v[:, cols(n)]
            base[n] = dy_v[:, cols(n)].astype(F32) + qg[...] * side[...]
            whole(m, n).wait_recv()
            gate_grad = (coef[n] * take(m, n)).astype(BF16)
            e = dot_nt(gate_grad, wg_v[:, cols(n)])
            base[n] += qg[...] * e
            acc[...] += jnp.sum(e * gx[...], axis=-1, keepdims=True)

        each(part)
        q = q_v[t]
        acc[...] = q * q * q * (acc[...] * (1.0 / model))

    def passing(n):
        return pltpu.make_async_remote_copy(
            src_ref=res.at[n],
            dst_ref=dyn.at[n],
            send_sem=psend.at[n],
            recv_sem=precv.at[n],
            device_id={"pipe": before},
            device_id_type=MESH,
        )

    finish(0, M0, V0)

    def hand_on(n):
        value = (base[n] - acc[...] * x0_v[:, cols(n)].astype(F32)).astype(BF16)
        res[n] = value
        passing(n).start()
        out0[:, cols(n)] = value

    each(hand_on)

    loads[9].wait()
    last = pi == npipe - 1

    def start1(n):
        passing(n).wait_recv()
        dy = jnp.where(last, lg_v[:, cols(n)].astype(F32), dyn[n].astype(F32)).astype(BF16)
        dy_v[:, cols(n)] = dy
        inner = dot_nt(dy, wo_v[:, cols(n)])
        put(G1, n, inner * silu[n])
        coef[n] = inner * slope[n]
        send(G1, n)

        @pl.when(n < NBLK - HELD)
        def _():
            mix(A1, M1, n)

    each(start1)
    each(functools.partial(fold, G1, V1))
    each(functools.partial(mix, A1, M1), NBLK - HELD)

    def drain(a, n):
        whole(a, n).wait_send()

    for a in (A0, G0, M0, V0, A1, G1, V1):
        each(functools.partial(drain, a))
    each(lambda n: passing(n).wait_send())
    finish(1, M1, V1)
    weight[...] = jnp.broadcast_to(acc[...], weight.shape)
    each(functools.partial(drain, M1))


def closing(out0, x1_v, base, weight, out_h, res, out_sem):
    width = base.shape[2]
    first = pltpu.make_async_copy(out0, out_h.at[0, 0], out_sem.at[NBLK])
    first.start()
    copies = []
    for n in range(NBLK):
        span = pl.ds(n * width, width)
        value = base[n] - weight[:, :1] * x1_v[:, span].astype(F32)
        res[n] = value.astype(BF16)
        copies.append(pltpu.make_async_copy(res.at[n], out_h.at[0, 1, :, span], out_sem.at[n]))
        copies[-1].start()
    for c in copies:
        c.wait()
    first.wait()


def local(*args):
    saved, _, _, _, w_gate, _, _, r_factor, l_factor = args
    _, ticks, rows, model = saved.shape
    width = w_gate.shape[1]
    nseq = lax.axis_size("seq")
    per = rows // nseq
    anywhere = pl.BlockSpec(memory_space=pl.ANY)
    vmem = pltpu.VMEM
    dma = pltpu.SemaphoreType.DMA
    parts = pl.pallas_call(
        kernel,
        out_shape=(
            vmem((rows, model), BF16),
            vmem((rows, model), BF16),
            vmem((NBLK, rows, width), F32),
            vmem((rows, 128), F32),
        ),
        in_specs=[anywhere] * len(args),
        out_specs=(pl.BlockSpec(memory_space=vmem),) * 4,
        scratch_shapes=[
            vmem((rows, model), BF16),
            vmem((rows, model), BF16),
            vmem((rows, model), BF16),
            vmem((1, model), F32),
            vmem((width, model), BF16),
            vmem((width, model), BF16),
            vmem((width, model), BF16),
            vmem((rows, rows), BF16),
            vmem((rows, rows), BF16),
            vmem(l_factor.shape[1:], BF16),
            vmem((rows, rows), BF16),
            vmem((rows, rows), BF16),
            vmem((8, NBLK, nseq, per, width), BF16),
            vmem((8, NBLK, nseq, per, width), BF16),
            vmem((NBLK, rows, width), F32),
            vmem((NBLK, rows, width), F32),
            vmem((NBLK, rows, width), F32),
            vmem((rows, width), F32),
            vmem((rows, width), F32),
            vmem((rows, width), F32),
            vmem((ticks, rows, 1), F32),
            vmem((rows, 1), F32),
            vmem((NBLK, rows, width), BF16),
            vmem((NBLK, rows, width), BF16),
            dma((10,)),
            dma((8, NBLK)),
            dma((8, NBLK)),
            dma((NBLK,)),
            dma((NBLK,)),
        ],
        compiler_params=pltpu.CompilerParams(
            collective_id=0, has_side_effects=True, vmem_limit_bytes=60 * 2**20
        ),
    )(*args)
    return pl.pallas_call(
        closing,
        out_shape=jax.ShapeDtypeStruct(saved.shape, BF16),
        in_specs=[pl.BlockSpec(memory_space=vmem)] * 4,
        out_specs=anywhere,
        scratch_shapes=[vmem((NBLK, rows, width), BF16), dma((NBLK + 1,))],
        compiler_params=pltpu.CompilerParams(vmem_limit_bytes=16 * 2**20),
    )(*parts)


def solution(mesh):
    placed = (
        P("pipe", None, "seq", None),
        P("pipe", "seq", None),
        P(None, "seq", None),
        P("pipe", None),
        P("pipe", None, None),
        P("pipe", None, None),
        P("pipe", None, None),
        P("pipe", "seq", None),
        P("pipe", "seq", None),
    )
    return jax.shard_map(
        local, mesh=mesh, in_specs=placed, out_specs=P("pipe", None, "seq", None), check_vma=False
    )
```

```python
import functools

import jax
import jax.numpy as jnp
from jax import lax
from jax.experimental import pallas as pl
from jax.experimental.pallas import tpu as pltpu
from jax.sharding import PartitionSpec as P

TICKS = 2
NBLK = 4
HELD = 2
NEAR = 3
MESH = pl.DeviceIdType.MESH
F32 = jnp.float32
BF16 = jnp.bfloat16

epsilon = 1e-05

A0, G0, M0, V0, A1, G1, M1, V1 = range(8)


def dot_nn(a, b):
    return lax.dot_general(a, b, (((1,), (0,)), ((), ())), preferred_element_type=F32)


def dot_nt(a, b):
    return lax.dot_general(a, b, (((1,), (1,)), ((), ())), preferred_element_type=F32)


def kernel(
    x_h, dy_h, lg_h, gain_h, wg_h, wv_h, wo_h, r_h, l_h,
    out0, x1_v, base, weight,
    x0_v, dy_v, lg_v, gain_v, wg_v, wv_v, wo_v, r_v, rt_v, l_v, lb_v, lbt_v,
    src, dst, coef, silu, slope, side, gx, qg, q_v, acc, res, dyn,
    load_sem, send_sem, recv_sem, psend, precv,
):
    nseq = lax.axis_size("seq")
    npipe = lax.axis_size("pipe")
    me = lax.axis_index("seq")
    pi = lax.axis_index("pipe")
    before = lax.rem(pi + npipe - 1, npipe)
    after = lax.rem(pi + 1, npipe)
    width = wg_v.shape[0]
    rows = r_v.shape[0]
    per = rows // nseq
    model = gain_v.shape[1]

    x_v = (x0_v, x1_v)
    pairs = (
        (x_h.at[0, 0], x0_v),
        (wv_h.at[0], wv_v),
        (r_h.at[0], r_v),
        (gain_h, gain_v),
        (wg_h.at[0], wg_v),
        (wo_h.at[0], wo_v),
        (dy_h.at[0], dy_v),
        (l_h.at[0], l_v),
        (x_h.at[0, 1], x1_v),
        (lg_h.at[0], lg_v),
    )
    loads = [pltpu.make_async_copy(a, b, load_sem.at[i]) for i, (a, b) in enumerate(pairs)]
    for c in loads[:4]:
        c.start()

    barrier = pltpu.get_barrier_semaphore()

    for d in range(nseq // 2, 0, -1):
        for peer in sorted({(nseq + d) % nseq, (nseq - d) % nseq}):
            pl.semaphore_signal(
                barrier, inc=1, device_id={"seq": lax.rem(me + peer, nseq)}, device_id_type=MESH
            )
    for other in (before, after):
        pl.semaphore_signal(barrier, inc=1, device_id={"pipe": other}, device_id_type=MESH)
    for c in loads[4:]:
        c.start()

    def copy_to(a, n, peer):
        return pltpu.make_async_remote_copy(
            src_ref=src.at[a, n, peer],
            dst_ref=dst.at[a, n, me],
            send_sem=send_sem.at[a, n],
            recv_sem=recv_sem.at[a, n],
            device_id={"seq": peer},
            device_id_type=MESH,
        )

    def send(a, n):
        half = nseq // 2

        def body(j, carry):
            copy_to(a, n, lax.rem(me + half + j, nseq)).start()
            copy_to(a, n, lax.rem(me + half - j, nseq)).start()
            return carry

        lax.fori_loop(half - NEAR, half, body, 0)
        copy_to(a, n, lax.rem(me + half, nseq)).start()
        lax.fori_loop(1, half - NEAR, body, 0)
        dst[a, n, me] = src[a, n, me]

    def whole(a, n):
        return pltpu.make_async_remote_copy(
            src_ref=src.at[a, n, pl.ds(0, nseq - 1)],
            dst_ref=dst.at[a, n, pl.ds(0, nseq - 1)],
            send_sem=send_sem.at[a, n],
            recv_sem=recv_sem.at[a, n],
            device_id={"seq": lax.rem(me + 1, nseq)},
            device_id_type=MESH,
        )

    def put(a, n, value):
        src[a, n] = value.reshape(nseq, per, width).astype(BF16)

    def take(a, n):
        return dst[a, n].astype(F32).reshape(rows, width)

    def cols(n):
        return pl.ds(pl.multiple_of(n * width, 128), width)

    def each(body, first=0):
        def step(n, carry):
            body(n)
            return carry

        lax.fori_loop(first, NBLK, step, 0)

    def scale_of(t):
        total = jnp.zeros((rows, 1), F32)
        for n in range(NBLK):
            v = x_v[t][:, n * width : (n + 1) * width].astype(F32)
            total = total + jnp.sum(v * v, axis=-1, keepdims=True)
        q_v[t] = lax.rsqrt(total * (1.0 / model) + epsilon)

    def normed_of(t, n):
        return (x_v[t][:, cols(n)].astype(F32) * q_v[t] * gain_v[:, cols(n)]).astype(BF16)

    for i in range(4):
        loads[i].wait()
    scale_of(0)

    def front0(n):
        normed = normed_of(0, n)
        values = dot_nn(normed, wv_v[:, cols(n)]).astype(BF16)
        put(A0, n, dot_nn(r_v[...], values))

    def back0(n):
        normed = normed_of(0, n)
        gate = dot_nn(normed, wg_v[:, cols(n)])
        inner = dot_nt(dy_v[:, cols(n)], wo_v[:, cols(n)])
        sig = jax.nn.sigmoid(gate)
        put(G0, n, inner * gate * sig)
        coef[n] = inner * (sig * (1.0 + gate * (1.0 - sig)))

    front0(0)
    pl.semaphore_wait(barrier, nseq + 1)
    send(A0, 0)
    for i in range(4, 7):
        loads[i].wait()

    def start0(n):
        @pl.when(n > 0)
        def _():
            front0(n)
            send(A0, n)

        back0(n)
        send(G0, n)

    each(start0)

    loads[7].wait()
    rt_v[...] = r_v[...].astype(F32).T.astype(BF16)
    wide = l_v.shape[1]
    tiled = jnp.broadcast_to(l_v[...].astype(F32)[None], (nseq, per, wide)).reshape(rows, wide)
    row = lax.broadcasted_iota(jnp.int32, (rows, wide), 0)
    col = lax.broadcasted_iota(jnp.int32, (rows, wide), 1)
    own = jnp.where(col // nseq == row // per, tiled, 0.0).astype(BF16)
    col_c = lax.broadcasted_iota(jnp.int32, (wide, rows), 0)
    row_c = lax.broadcasted_iota(jnp.int32, (wide, rows), 1)
    spread = jnp.where(col_c % nseq == row_c // per, 1.0, 0.0).astype(BF16)
    big = dot_nn(own, spread)
    ra = lax.broadcasted_iota(jnp.int32, (rows, rows), 0)
    rb = lax.broadcasted_iota(jnp.int32, (rows, rows), 1)
    big = jnp.where(ra % per == rb % per, big, 0.0)
    lb_v[...] = big.astype(BF16)
    lbt_v[...] = big.T.astype(BF16)

    loads[8].wait()
    scale_of(1)

    def front1(n):
        normed = normed_of(1, n)
        values = dot_nn(normed, wv_v[:, cols(n)]).astype(BF16)
        put(A1, n, dot_nn(r_v[...], values))
        gate = dot_nn(normed, wg_v[:, cols(n)])
        sig = jax.nn.sigmoid(gate)
        silu[n] = gate * sig
        slope[n] = sig * (1.0 + gate * (1.0 - sig))

    each(front1)

    def mix(a, b, n):
        whole(a, n).wait_recv()
        put(b, n, dot_nn(lb_v[...], take(a, n).astype(BF16)))
        send(b, n)

    def fold(a, b, n):
        whole(a, n).wait_recv()
        put(b, n, dot_nn(lbt_v[...], take(a, n).astype(BF16)))
        send(b, n)

    def turn0(n):
        mix(A0, M0, n)
        fold(G0, V0, n)

    each(turn0)
    each(functools.partial(send, A1))

    def finish(t, m, v):
        acc[...] = jnp.zeros_like(acc)

        def part(n):
            whole(v, n).wait_recv()
            value_grad = dot_nn(rt_v[...], take(v, n).astype(BF16)).astype(BF16)
            side[...] = dot_nt(value_grad, wv_v[:, cols(n)])
            scaled = gain_v[:, cols(n)] * x_v[t][:, cols(n)].astype(F32)
            gx[...] = scaled
            acc[...] += jnp.sum(side[...] * scaled, axis=-1, keepdims=True)
            qg[...] = q_v[t] * gain_v[:, cols(n)]
            base[n] = dy_v[:, cols(n)].astype(F32) + qg[...] * side[...]
            whole(m, n).wait_recv()
            gate_grad = (coef[n] * take(m, n)).astype(BF16)
            e = dot_nt(gate_grad, wg_v[:, cols(n)])
            base[n] += qg[...] * e
            acc[...] += jnp.sum(e * gx[...], axis=-1, keepdims=True)

        each(part)
        q = q_v[t]
        acc[...] = q * q * q * (acc[...] * (1.0 / model))

    def passing(n):
        return pltpu.make_async_remote_copy(
            src_ref=res.at[n],
            dst_ref=dyn.at[n],
            send_sem=psend.at[n],
            recv_sem=precv.at[n],
            device_id={"pipe": before},
            device_id_type=MESH,
        )

    finish(0, M0, V0)

    def hand_on(n):
        value = (base[n] - acc[...] * x0_v[:, cols(n)].astype(F32)).astype(BF16)
        res[n] = value
        passing(n).start()
        out0[:, cols(n)] = value

    each(hand_on)

    loads[9].wait()
    last = pi == npipe - 1

    def start1(n):
        passing(n).wait_recv()
        dy = jnp.where(last, lg_v[:, cols(n)].astype(F32), dyn[n].astype(F32)).astype(BF16)
        dy_v[:, cols(n)] = dy
        inner = dot_nt(dy, wo_v[:, cols(n)])
        put(G1, n, inner * silu[n])
        coef[n] = inner * slope[n]
        send(G1, n)

        @pl.when(n < NBLK - HELD)
        def _():
            mix(A1, M1, n)

    each(start1)
    each(functools.partial(fold, G1, V1))
    each(functools.partial(mix, A1, M1), NBLK - HELD)

    def drain(a, n):
        whole(a, n).wait_send()

    for a in (A0, G0, M0, V0, A1, G1, V1):
        each(functools.partial(drain, a))
    each(lambda n: passing(n).wait_send())
    finish(1, M1, V1)
    weight[...] = jnp.broadcast_to(acc[...], weight.shape)
    each(functools.partial(drain, M1))


def closing(out0, x1_v, base, weight, out_h, res, out_sem):
    width = base.shape[2]
    first = pltpu.make_async_copy(out0, out_h.at[0, 0], out_sem.at[NBLK])
    first.start()
    copies = []
    for n in range(NBLK):
        span = pl.ds(n * width, width)
        value = base[n] - weight[:, :1] * x1_v[:, span].astype(F32)
        res[n] = value.astype(BF16)
        copies.append(pltpu.make_async_copy(res.at[n], out_h.at[0, 1, :, span], out_sem.at[n]))
        copies[-1].start()
    for c in copies:
        c.wait()
    first.wait()


def local(*args):
    saved, _, _, _, w_gate, _, _, r_factor, l_factor = args
    _, ticks, rows, model = saved.shape
    width = w_gate.shape[1]
    nseq = lax.axis_size("seq")
    per = rows // nseq
    anywhere = pl.BlockSpec(memory_space=pl.ANY)
    vmem = pltpu.VMEM
    dma = pltpu.SemaphoreType.DMA
    parts = pl.pallas_call(
        kernel,
        out_shape=(
            vmem((rows, model), BF16),
            vmem((rows, model), BF16),
            vmem((NBLK, rows, width), F32),
            vmem((rows, 128), F32),
        ),
        in_specs=[anywhere] * len(args),
        out_specs=(pl.BlockSpec(memory_space=vmem),) * 4,
        scratch_shapes=[
            vmem((rows, model), BF16),
            vmem((rows, model), BF16),
            vmem((rows, model), BF16),
            vmem((1, model), F32),
            vmem((width, model), BF16),
            vmem((width, model), BF16),
            vmem((width, model), BF16),
            vmem((rows, rows), BF16),
            vmem((rows, rows), BF16),
            vmem(l_factor.shape[1:], BF16),
            vmem((rows, rows), BF16),
            vmem((rows, rows), BF16),
            vmem((8, NBLK, nseq, per, width), BF16),
            vmem((8, NBLK, nseq, per, width), BF16),
            vmem((NBLK, rows, width), F32),
            vmem((NBLK, rows, width), F32),
            vmem((NBLK, rows, width), F32),
            vmem((rows, width), F32),
            vmem((rows, width), F32),
            vmem((rows, width), F32),
            vmem((ticks, rows, 1), F32),
            vmem((rows, 1), F32),
            vmem((NBLK, rows, width), BF16),
            vmem((NBLK, rows, width), BF16),
            dma((10,)),
            dma((8, NBLK)),
            dma((8, NBLK)),
            dma((NBLK,)),
            dma((NBLK,)),
        ],
        compiler_params=pltpu.CompilerParams(
            collective_id=0, has_side_effects=True, vmem_limit_bytes=60 * 2**20
        ),
    )(*args)
    return pl.pallas_call(
        closing,
        out_shape=jax.ShapeDtypeStruct(saved.shape, BF16),
        in_specs=[pl.BlockSpec(memory_space=vmem)] * 4,
        out_specs=anywhere,
        scratch_shapes=[vmem((NBLK, rows, width), BF16), dma((NBLK + 1,))],
        compiler_params=pltpu.CompilerParams(vmem_limit_bytes=16 * 2**20),
    )(*parts)


def solution(mesh):
    placed = (
        P("pipe", None, "seq", None),
        P("pipe", "seq", None),
        P(None, "seq", None),
        P("pipe", None),
        P("pipe", None, None),
        P("pipe", None, None),
        P("pipe", None, None),
        P("pipe", "seq", None),
        P("pipe", "seq", None),
    )
    return jax.shard_map(
        local, mesh=mesh, in_specs=placed, out_specs=P("pipe", None, "seq", None), check_vma=False
    )
```
